256 devices in a mesh: dp: 16 (over z_hi, x, core), row: 4 (over y), col: 4 (over z_lo).
Axes of the slice: x: 4, y: 4, z: 8 (z_hi: 2, z_lo: 4; z = z_hi * 4 + z_lo), core: 2. Of those that a mesh axis runs over, the one named last changes fastest.
Arguments:
- grad_parts: float32 [16, 2, 4096, 5120], P('dp', None, 'row', 'col'), may hold values from -5 to 5
- weight: float32 [2, 4096, 5120], P(None, ('row', 'dp'), 'col'), may hold values from -6 to 6
- row_state: float32 [2, 4096], P(None, ('row', 'dp')), may hold values from 0.3 to 8, as said below
- col_state: float32 [2, 5120], P(None, 'col'), may hold values from 0.05 to 0.5
Outputs:
- new_weight: float32 [2, 4096, 5120], P(None, 'row', 'col')
- new_row_state: float32 [2, 4096], P(None, ('row', 'dp'))
- new_col_state: float32 [2, 5120], P(None, 'col')
The draws below stay inside these ranges and needn't reach their ends.
Inputs may be any that keep to these rules, and one draw needn't show every extreme that they name: `row_state`: positive row moments.
All inputs are finite; a program needn't handle non-finite values.
Results may differ from the reference program's by a relative error of at most 0.00002.
Values sent between devices are 32-bit elements; how exact they have to be, the bound alone decides.
No kernel may reach another device: no remote copies, remote signals or barrier semaphores. Data moves between devices by JAX's collectives and lax.ppermute only.
A program may use at most 128 MiB of HBM per device.

```python
import math
import jax
import jax.numpy as jnp
from jax import lax

D = 4096
FF = 5120
EXPERTS = 2
N_DP = 16
N_ROW = 4


def draw_row_state(key, part):
    rows = jnp.arange(D)
    block = D // (N_ROW * N_DP)
    replica = rows // block % N_DP
    level = replica.astype(jnp.float32) / max(N_DP - 1, 1)
    base = 0.5 * 10.0 ** level
    jitter = jnp.exp(jax.random.uniform(key, (EXPERTS, D), jnp.float32, jnp.log(0.7), jnp.log(1.4)))
    return (base[None, :] * jitter).astype(jnp.float32)


def raised(array, stream_key, source, target, shards_of, factor):
    owner, partner = [(jnp.arange(array.shape[axis_at]) // (array.shape[axis_at] // shards_of)).reshape([-1 if axis == axis_at else 1 for axis in range(array.ndim)]) for axis_at in (source, target)]
    chosen = jax.random.permutation(stream_key, shards_of)[partner]
    strong = (owner == chosen) | (owner == (partner + shards_of // 2) % shards_of)
    return jnp.where(strong, factor * array, array)


def block_levels(stream_key, dims, split, least, largest):
    loudness = 1.0
    for dim, shards_of in split:
        steps = jax.random.uniform(jax.random.fold_in(jax.random.fold_in(stream_key, 6), dim), (shards_of,), jnp.float32, least / len(split), largest / len(split))
        loudness = loudness * jnp.repeat(jnp.exp(steps), dims[dim] // shards_of).reshape((-1,) + (1,) * (len(dims) - 1 - dim))
    return loudness


def gaussian(key, shape, deviation, bound, split=(), dtype=jnp.bfloat16):
    array = jax.random.normal(key, shape, jnp.float32) * deviation
    if len(split) > 0:
        array = block_levels(key, shape, split, -0.22, 0.18) * array
    return jnp.clip(array, min=-bound, max=bound).astype(dtype)


def gaussian_with(rng, dims, width, most, pieces, heavy, held_as=jnp.bfloat16):
    drawn = width * jax.random.normal(rng, dims, jnp.float32)
    if pieces:
        drawn = drawn * block_levels(rng, dims, pieces, -0.22, 0.18)
    return jnp.clip(raised(drawn, jax.random.fold_in(rng, 3), *heavy), -most, most).astype(held_as)


def setup_inputs(seed: int = 0) -> dict:
    seeds = jax.random.split(jax.random.key(seed), 5)
    grad_parts = gaussian_with(seeds[0], (N_DP, EXPERTS, D, FF), (1.0 / N_DP ** 0.5), 5.0, ((0, 16), (2, 4), (3, 4)), (0, 2, 16, 2.0), jnp.float32)
    weight = gaussian(seeds[1], (EXPERTS, D, FF), 1.0, 6.0, ((1, 64), (2, 4)), jnp.float32)
    row_state = draw_row_state(jax.random.fold_in(seeds[4], 71), 0)
    col_state = jnp.clip(jnp.exp(math.log(0.5) - 2.3025851 * jax.random.uniform(seeds[3], (EXPERTS, FF), jnp.float32) ** block_levels(seeds[3], (EXPERTS, FF), ((1, 4),), -0.2, 0.2)), 0.05, 0.5)
    return {"grad_parts": grad_parts, "weight": weight, "row_state": row_state, "col_state": col_state}


def reference(grad_parts, weight, row_state, col_state):
    decay = 1.0 - 2.0 ** (-0.8)
    grad = lax.optimization_barrier(jnp.sum(grad_parts, axis=0))
    sq = grad * grad + 1e-30
    new_row = decay * row_state + (1.0 - decay) * lax.optimization_barrier(jnp.sum(sq, axis=2)) / FF
    new_col = decay * col_state + (1.0 - decay) * lax.optimization_barrier(jnp.sum(sq, axis=1)) / D
    row_mean = lax.optimization_barrier(jnp.sum(new_row, axis=1)) / D
    vhat = new_row[:, :, None] * new_col[:, None, :] / row_mean[:, None, None]
    update = grad / jnp.sqrt(vhat)
    clip = jnp.maximum(1.0, jnp.sqrt(lax.optimization_barrier(jnp.sum(update * update, axis=(1, 2))) / (D * FF)))
    step_size = 0.3 * jnp.maximum(0.001, jnp.sqrt(lax.optimization_barrier(jnp.sum(weight * weight, axis=(1, 2))) / (D * FF)))
    new_weight = weight - (step_size / clip)[:, None, None] * update
    return (new_weight, new_row, new_col)
```

```python
import functools

import jax
import jax.numpy as jnp
from jax import lax
from jax.experimental import pallas as pl
from jax.experimental.pallas import tpu as pltpu
from jax.sharding import PartitionSpec as P

D = 4096
FF = 5120
E = 2
ROWS = 64
COLS = 1280
DECAY = 1.0 - 2.0 ** (-0.8)

DP = [(zh, x, c) for zh in range(2) for x in range(4) for c in range(2)]


def at(zh, x, c):
    return (zh % 2) * 8 + (x % 4) * 2 + c % 2


def dp_perm(dz, dx, dc):
    return [(at(zh, x, c), at(zh + dz, x + dx, c + dc)) for zh, x, c in DP]


CORE = dp_perm(0, 0, 1)
PLUS = dp_perm(0, 1, 0)
MINUS = dp_perm(0, -1, 0)
ZHALF = dp_perm(1, 0, 0)


def send(value, perm):
    return lax.ppermute(value, "dp", perm)


def sum4(value, axis, perms):
    second, third, fourth = (lax.ppermute(value, axis, perm) for perm in perms)
    return (value + third) + (second + fourth)


RING4 = [[(i, (i + k) % 4) for i in range(4)] for k in (1, 2, 3)]
X4 = [dp_perm(0, k, 0) for k in (1, 2, 3)]


def place():
    dp = lax.axis_index("dp")
    return dp // 8, dp // 2 % 4, dp % 2


def swap_half(parts, expert):
    _, _, c = place()
    theirs = lax.dynamic_slice(
        parts, (expert, 0, 0, 1 - c, 0, 0), (1, 2, 4, 1, ROWS, COLS)
    )
    return send(theirs.reshape(2, 4, ROWS, COLS), CORE)


def scatter_x(parts, other, expert):
    _, x, c = place()

    def block(half, dx):
        at_x = (x + dx) % 4
        mine = lax.dynamic_slice(
            parts, (expert, half, at_x, c, 0, 0), (1, 1, 1, 1, ROWS, COLS)
        )
        theirs = lax.dynamic_slice(other, (half, at_x, 0, 0), (1, 1, ROWS, COLS))
        return mine.reshape(ROWS, COLS) + theirs.reshape(ROWS, COLS)

    pick = [(0, 2), (1, 2), (1, 1), (0, 3), (0, 1), (1, 3), (0, 0), (1, 0)]
    far_a, far_b, near_b, near_a, next_a, next_b, own_a, own_b = lax.optimization_barrier(
        [block(*p) for p in pick]
    )
    far_a = send(far_a, PLUS)
    far_b = send(far_b, MINUS)
    near_b = send(near_b, PLUS)
    near_a = send(near_a, MINUS)
    both_a = send(next_a + far_a, PLUS)
    both_b = send(next_b + far_b, MINUS)
    return own_a + near_a + both_a, own_b + near_b + both_b


def scatter_z(total_a, total_b):
    zh, _, _ = place()
    away = send(jnp.where(zh == 0, total_b, total_a), ZHALF)
    return jnp.where(zh == 0, total_a, total_b) + away


def statistics(grad, weight, row_state, col_state):
    sq = grad * grad + 1e-30
    row_total = sum4(jnp.sum(sq, axis=2), "col", RING4)
    row = DECAY * row_state + (1.0 - DECAY) * row_total / FF
    sums = jnp.concatenate(
        [
            jnp.sum(sq, axis=1),
            jnp.sum(grad * grad / row[:, :, None], axis=1),
            jnp.sum(weight * weight, axis=1),
            jnp.broadcast_to(jnp.sum(row, axis=1)[:, None], (E, COLS)),
        ]
    )
    sums = sum4(sums, "dp", X4)
    sums = sum4(sums, "row", RING4)
    sums = sums + send(sums, CORE)
    sums = sums + send(sums, ZHALF)
    squares, scaled, weights, rows = (sums[E * i : E * i + E] for i in range(4))
    col = DECAY * col_state + (1.0 - DECAY) * squares / D
    row_mean = rows[:, 0] / D
    scalars = jnp.stack([jnp.sum(scaled / col, axis=1), jnp.sum(weights, axis=1)])
    scalars = sum4(scalars, "col", RING4)
    clip = jnp.maximum(1.0, jnp.sqrt(scalars[0] * row_mean / (D * FF)))
    step = 0.3 * jnp.maximum(0.001, jnp.sqrt(scalars[1] / (D * FF)))
    return row, col, row_mean, step / clip


def place_kernel(count, where, *refs):
    blocks, out, held, loaded, stored = refs[:count], *refs[-4:]
    loads = [
        pltpu.make_async_copy(block, held.at[i], loaded.at[i])
        for i, block in enumerate(blocks)
    ]
    stores = [
        pltpu.make_async_copy(
            held.at[i], out.at[pl.ds(pl.multiple_of(where[i], ROWS), ROWS)], stored.at[i]
        )
        for i in range(count)
    ]
    for load in loads:
        load.start()
    for load, store in zip(loads, stores):
        load.wait()
        store.start()
    for store in stores:
        store.wait()


def put(out, blocks, rows):
    count = len(blocks)
    any_space = pl.BlockSpec(memory_space=pl.ANY)
    operands = [jnp.stack(rows).astype(jnp.int32), *blocks]
    specs = [pl.BlockSpec(memory_space=pltpu.SMEM)] + [any_space] * count
    aliases = {}
    if out is not None:
        operands.append(out)
        specs.append(any_space)
        aliases = {count + 1: 0}
    return pl.pallas_call(
        functools.partial(place_kernel, count),
        out_shape=jax.ShapeDtypeStruct((E * 1024, COLS), jnp.float32),
        in_specs=specs,
        out_specs=any_space,
        scratch_shapes=[
            pltpu.VMEM((count, ROWS, COLS), jnp.float32),
            pltpu.SemaphoreType.DMA((count,)),
            pltpu.SemaphoreType.DMA((count,)),
        ],
        input_output_aliases=aliases,
    )(*operands)


def gather_rows(shard):
    zh, x, c = place()

    def row(expert, dz, dx, dc):
        return expert * 1024 + ROWS * ((zh + dz) % 2 * 8 + (x + dx) % 4 * 2 + (c + dc) % 2)

    other = [send(s, ZHALF) for s in shard]
    pieces = []
    for dz, mine in ((0, shard), (1, other)):
        left = [send(m, PLUS) for m in mine]
        right = [send(m, MINUS) for m in mine]
        far = [send(left[0], PLUS), send(right[1], MINUS)]
        for dx, blocks in ((0, mine), (3, left), (1, right), (2, far)):
            pieces += [(block, e, dz, dx) for e, block in enumerate(blocks)]
    out = put(None, [p[0] for p in pieces], [row(*p[1:], 0) for p in pieces])
    swapped = [(send(p[0], CORE), *p[1:]) for p in pieces]
    return put(out, [p[0] for p in swapped], [row(*p[1:], 1) for p in swapped])


def body(grad_parts, weight, row_state, col_state):
    parts = grad_parts.reshape(E, 2, 4, 2, ROWS, COLS)
    others = [swap_half(parts, e) for e in range(E)]
    totals = [scatter_x(parts, others[e], e) for e in range(E)]
    grad = jnp.stack([scatter_z(*total) for total in totals])
    row, col, row_mean, scale = statistics(grad, weight, row_state, col_state)
    vhat = row[:, :, None] * col[:, None, :] / row_mean[:, None, None]
    new = weight - scale[:, None, None] * (grad / jnp.sqrt(vhat))
    return gather_rows(list(new)).reshape(E, 1024, COLS), row, col


def solution(mesh):
    placed = (
        P("dp", None, "row", "col"),
        P(None, ("row", "dp"), "col"),
        P(None, ("row", "dp")),
        P(None, "col"),
    )
    return jax.shard_map(
        body,
        mesh=mesh,
        in_specs=placed,
        out_specs=(P(None, "row", "col"), P(None, ("row", "dp")), P(None, "col")),
        check_vma=False,
    )
```

```python
import functools

import jax
import jax.numpy as jnp
from jax import lax
from jax.experimental import pallas as pl
from jax.experimental.pallas import tpu as pltpu
from jax.sharding import PartitionSpec as P

D = 4096
FF = 5120
E = 2
ROWS = 64
COLS = 1280
DECAY = 1.0 - 2.0 ** (-0.8)

DP = [(zh, x, c) for zh in range(2) for x in range(4) for c in range(2)]


def at(zh, x, c):
    return (zh % 2) * 8 + (x % 4) * 2 + c % 2


def dp_perm(dz, dx, dc):
    return [(at(zh, x, c), at(zh + dz, x + dx, c + dc)) for zh, x, c in DP]


CORE = dp_perm(0, 0, 1)
PLUS = dp_perm(0, 1, 0)
MINUS = dp_perm(0, -1, 0)
ZHALF = dp_perm(1, 0, 0)
FAR = dp_perm(0, 2, 0)


def send(value, perm):
    return lax.ppermute(value, "dp", perm)


def sum4(value, axis, perms):
    second, third, fourth = (lax.ppermute(value, axis, perm) for perm in perms)
    return (value + third) + (second + fourth)


RING4 = [[(i, (i + k) % 4) for i in range(4)] for k in (1, 2, 3)]
X4 = [dp_perm(0, k, 0) for k in (1, 2, 3)]


def place():
    dp = lax.axis_index("dp")
    return dp // 8, dp // 2 % 4, dp % 2


def after(values, *earlier):
    return lax.optimization_barrier((values, earlier))[0]


def cut(parts, start, size):
    return lax.dynamic_slice(parts, (*start, 0, 0), (*size, ROWS, COLS))


def scatter(parts):
    zh, x, c = place()
    high, low = x // 2, x % 2

    def swap(start, size, *earlier):
        core = after(1 - c, *earlier) if earlier else 1 - c
        return send(cut(parts, (*start, core), (*size, 1)), CORE)

    def block(theirs, expert, half, dx):
        to = (x + dx) % 4
        mine = cut(parts, (expert, half, to // 2, to % 2, c), (1,) * 5)
        return mine.reshape(ROWS, COLS) + theirs.reshape(ROWS, COLS)

    def block_pair(theirs, half, dxs):
        return [block(theirs[e], e, half, dxs[e]) for e in range(E)]

    def sides(swap, half, swapped):
        pick = lambda e, dx: lax.dynamic_index_in_dim(swap[e, 0], (x + dx) % 4 // 2, 0)
        order = (1, 0) if swapped else (0, 1)
        return [block(pick(e, dx), e, half, dx) for e, dx in zip(order, (1, 3))]

    def pair_send(pair):
        return [send(pair[0], PLUS), send(pair[1], MINUS)]

    def finish(far, side_swap, own_swap, half):
        near_rows = sides(side_swap, half, True)
        next_rows = sides(side_swap, half, False)
        rows = after(
            [jnp.concatenate([n, m + f]) for n, m, f in zip(near_rows, next_rows, far)]
        )
        got = pair_send(rows)
        own = block_pair(own_swap, half, (0, 0))
        total = [own[e] + got[1 - e][:ROWS] + got[e][ROWS:] for e in range(E)]
        return rows, after(jnp.stack(total))

    far_a = swap((0, 1 - zh, 1 - high, low), (E, 1, 1, 1))
    far_rows = after(block_pair(far_a, 1 - zh, (2, 2)))
    far = pair_send(far_rows)
    side_a = swap((0, 1 - zh, 0, 1 - low), (E, 1, 2, 1), far_rows)
    own_a = swap((0, 1 - zh, high, low), (E, 1, 1, 1), far_rows)
    rows, away = finish(far, side_a, own_a, 1 - zh)

    def both_experts(dx):
        to = (x + dx) % 4
        start = (0, zh, to // 2, to % 2)
        theirs = swap(start, (E, 1, 1, 1), rows)
        mine = cut(parts, (*start, c), (E, 1, 1, 1, 1))
        return (mine + theirs).reshape(E, ROWS, COLS)

    *terms, own = after([both_experts(dx) for dx in (1, 3, 2, 0)], rows)
    *terms, away = lax.optimization_barrier((*terms, away))
    other = send(away, ZHALF)
    got = [send(term, perm) for term, perm in zip(terms, (PLUS, MINUS, FAR))]
    return own + got[0] + got[1] + got[2] + other


def statistics(grad, weight, row_state, col_state):
    sq = grad * grad + 1e-30
    row_total = sum4(jnp.sum(sq, axis=2), "col", RING4)
    row = DECAY * row_state + (1.0 - DECAY) * row_total / FF
    sums = jnp.concatenate(
        [
            jnp.sum(sq, axis=1),
            jnp.sum(grad * grad / row[:, :, None], axis=1),
            jnp.sum(weight * weight, axis=1),
            jnp.broadcast_to(jnp.sum(row, axis=1)[:, None], (E, COLS)),
        ]
    )
    sums = sum4(sums, "dp", X4)
    sums = sum4(sums, "row", RING4)
    for perm in (CORE, ZHALF):
        sums = sums + send(sums, perm)
    squares, scaled, weights, rows = (sums[E * i : E * i + E] for i in range(4))
    col = DECAY * col_state + (1.0 - DECAY) * squares / D
    row_mean = rows[:, 0] / D
    scalars = jnp.stack([jnp.sum(scaled / col, axis=1), jnp.sum(weights, axis=1)])
    scalars = sum4(scalars, "col", RING4)
    clip = jnp.maximum(1.0, jnp.sqrt(scalars[0] * row_mean / (D * FF)))
    step = 0.3 * jnp.maximum(0.001, jnp.sqrt(scalars[1] / (D * FF)))
    return row, col, row_mean, step / clip


def place_kernel(slabs, where, *refs):
    *arrays, out, held, loaded, stored = refs
    copies = []
    at_row = 0
    for i, (array, start, size) in enumerate(slabs):
        stage = held.at[pl.ds(at_row, size)]
        at_row += size
        target = out.at[pl.ds(pl.multiple_of(where[i], 32), size)]
        copies.append(
            (
                pltpu.make_async_copy(arrays[array].at[pl.ds(start, size)], stage, loaded.at[i]),
                pltpu.make_async_copy(stage, target, stored.at[i]),
            )
        )
    for load, _ in copies:
        load.start()
    for load, store in copies:
        load.wait()
        store.start()
    for _, store in copies:
        store.wait()


def put(out, arrays, slabs, rows):
    any_space = pl.BlockSpec(memory_space=pl.ANY)
    operands = [jnp.stack(rows).astype(jnp.int32)]
    operands += [array.reshape(-1, COLS) for array in arrays]
    aliases = {}
    if out is not None:
        aliases = {len(operands): 0}
        operands.append(out)
    specs = [pl.BlockSpec(memory_space=pltpu.SMEM)] + [any_space] * (len(operands) - 1)
    return pl.pallas_call(
        functools.partial(place_kernel, slabs),
        out_shape=jax.ShapeDtypeStruct((E * 1024, COLS), jnp.float32),
        in_specs=specs,
        out_specs=any_space,
        scratch_shapes=[
            pltpu.VMEM((sum(size for _, _, size in slabs), COLS), jnp.float32),
            pltpu.SemaphoreType.DMA((len(slabs),)),
            pltpu.SemaphoreType.DMA((len(slabs),)),
        ],
        input_output_aliases=aliases,
    )(*operands)


def gather_rows(shard):
    zh, x, c = place()
    half = ROWS // 2

    def row(dc, expert, dz, dx, first=0):
        at_c = (zh + dz) % 2 * 8 + (x + dx) % 4 * 2 + (c + dc) % 2
        return expert * 1024 + ROWS * at_c + first

    def write(out, pieces):
        arrays, slabs, rows = [], [], []
        for mine, theirs, parts in pieces:
            for dc, array in enumerate((mine, theirs)):
                start = 0
                for size, *to in parts:
                    slabs.append((len(arrays), start, size))
                    rows.append(row(dc, *to))
                    start += size
                arrays.append(array)
        return put(out, arrays, slabs, rows)

    other = [send(shard[e], ZHALF) for e in range(E)]
    left, right = send(shard, PLUS), send(shard, MINUS)
    shard_c = send(shard, CORE)

    left, right, other_0, shard_c = lax.optimization_barrier((left, right, other[0], shard_c))
    plus = jnp.concatenate([left[0], other_0])
    minus = jnp.concatenate([right[1], other_0])
    plus, minus = lax.optimization_barrier((plus, minus))
    from_left, from_right = send(plus, PLUS), send(minus, MINUS)
    left_c, right_c = send(left, CORE), send(right, CORE)

    from_left, from_right, other_1, left_c, right_c = lax.optimization_barrier(
        (from_left, from_right, other[1], left_c, right_c)
    )
    plus = jnp.concatenate([other_1, from_left[ROWS : ROWS + half]])
    minus = jnp.concatenate([other_1, from_right[ROWS + half :]])
    plus, minus = lax.optimization_barrier((plus, minus))
    last_left, last_right = send(plus, PLUS), send(minus, MINUS)
    far_1 = send(other_1, FAR)
    from_left_c, from_right_c = send(from_left, CORE), send(from_right, CORE)
    others = jnp.concatenate([other_0, other_1])
    both = lambda dz, dx: [(ROWS, e, dz, dx) for e in range(E)]
    out = write(
        None,
        [
            (shard, shard_c, both(0, 0)),
            (left, left_c, both(0, 3)),
            (right, right_c, both(0, 1)),
            (from_left, from_left_c, [(ROWS, 0, 0, 2), (ROWS, 0, 1, 3)]),
            (from_right, from_right_c, [(ROWS, 1, 0, 2), (ROWS, 0, 1, 1)]),
        ],
    )

    out, last_left, last_right, far_1, others = lax.optimization_barrier(
        (out, last_left, last_right, far_1, others)
    )
    return write(
        out,
        [
            (others, send(others, CORE), both(1, 0)),
            (last_left, send(last_left, CORE), [(ROWS, 1, 1, 3), (half, 0, 1, 2, 0)]),
            (last_right, send(last_right, CORE), [(ROWS, 1, 1, 1), (half, 0, 1, 2, half)]),
            (far_1, send(far_1, CORE), [(ROWS, 1, 1, 2)]),
        ],
    )


def body(grad_parts, weight, row_state, col_state):
    grad = scatter(grad_parts.reshape(E, 2, 2, 2, 2, ROWS, COLS))
    row, col, row_mean, scale = statistics(grad, weight, row_state, col_state)
    vhat = row[:, :, None] * col[:, None, :] / row_mean[:, None, None]
    new = weight - scale[:, None, None] * (grad / jnp.sqrt(vhat))
    return gather_rows(new).reshape(E, 1024, COLS), row, col


def solution(mesh):
    placed = (
        P("dp", None, "row", "col"),
        P(None, ("row", "dp"), "col"),
        P(None, ("row", "dp")),
        P(None, "col"),
    )
    return jax.shard_map(
        body,
        mesh=mesh,
        in_specs=placed,
        out_specs=(P(None, "row", "col"), P(None, ("row", "dp")), P(None, "col")),
        check_vma=False,
    )
```

```python
import functools

import jax
import jax.numpy as jnp
from jax import lax
from jax.experimental import pallas as pl
from jax.experimental.pallas import tpu as pltpu
from jax.sharding import PartitionSpec as P

D = 4096
FF = 5120
E = 2
ROWS = 64
COLS = 1280
DECAY = 1.0 - 2.0 ** (-0.8)

DP = [(zh, x, c) for zh in range(2) for x in range(4) for c in range(2)]


def at(zh, x, c):
    return (zh % 2) * 8 + (x % 4) * 2 + c % 2


def dp_perm(dz, dx, dc):
    return [(at(zh, x, c), at(zh + dz, x + dx, c + dc)) for zh, x, c in DP]


CORE = dp_perm(0, 0, 1)
PLUS = dp_perm(0, 1, 0)
MINUS = dp_perm(0, -1, 0)
ZHALF = dp_perm(1, 0, 0)
FAR = dp_perm(0, 2, 0)


def send(value, perm):
    return lax.ppermute(value, "dp", perm)


def sum4(value, axis, perms):
    second, third, fourth = (lax.ppermute(value, axis, perm) for perm in perms)
    return (value + third) + (second + fourth)


RING4 = [[(i, (i + k) % 4) for i in range(4)] for k in (1, 2, 3)]
X4 = [dp_perm(0, k, 0) for k in (1, 2, 3)]


def place():
    dp = lax.axis_index("dp")
    return dp // 8, dp // 2 % 4, dp % 2


def after(values, *earlier):
    return lax.optimization_barrier((values, earlier))[0]


def cut(parts, start, size):
    return lax.dynamic_slice(parts, (*start, 0, 0), (*size, ROWS, COLS))


def scatter(parts):
    zh, x, c = place()
    high, low = x // 2, x % 2

    def swap(start, size, *earlier):
        core = after(1 - c, *earlier) if earlier else 1 - c
        return send(cut(parts, (*start, core), (*size, 1)), CORE)

    def block(theirs, expert, half, dx):
        to = (x + dx) % 4
        mine = cut(parts, (expert, half, to // 2, to % 2, c), (1,) * 5)
        return mine.reshape(ROWS, COLS) + theirs.reshape(ROWS, COLS)

    def block_pair(theirs, half, dxs):
        return [block(theirs[e], e, half, dxs[e]) for e in range(E)]

    def sides(swap, half, swapped):
        pick = lambda e, dx: lax.dynamic_index_in_dim(swap[e, 0], (x + dx) % 4 // 2, 0)
        order = (1, 0) if swapped else (0, 1)
        return [block(pick(e, dx), e, half, dx) for e, dx in zip(order, (1, 3))]

    def pair_send(pair):
        return [send(pair[0], PLUS), send(pair[1], MINUS)]

    def finish(far, side_swap, own_swap, half):
        near_rows = sides(side_swap, half, True)
        next_rows = sides(side_swap, half, False)
        rows = after(
            [jnp.concatenate([n, m + f]) for n, m, f in zip(near_rows, next_rows, far)]
        )
        got = pair_send(rows)
        own = block_pair(own_swap, half, (0, 0))
        total = [own[e] + got[1 - e][:ROWS] + got[e][ROWS:] for e in range(E)]
        return rows, after(jnp.stack(total))

    far_a = swap((0, 1 - zh, 1 - high, low), (E, 1, 1, 1))
    far_rows = after(block_pair(far_a, 1 - zh, (2, 2)))
    far = pair_send(far_rows)
    side_a = swap((0, 1 - zh, 0, 1 - low), (E, 1, 2, 1), far_rows)
    own_a = swap((0, 1 - zh, high, low), (E, 1, 1, 1), far_rows)
    rows, away = finish(far, side_a, own_a, 1 - zh)

    def both_experts(dx):
        to = (x + dx) % 4
        start = (0, zh, to // 2, to % 2)
        theirs = swap(start, (E, 1, 1, 1), rows)
        mine = cut(parts, (*start, c), (E, 1, 1, 1, 1))
        return (mine + theirs).reshape(E, ROWS, COLS)

    *terms, own = after([both_experts(dx) for dx in (1, 3, 2, 0)], rows)
    *terms, away = lax.optimization_barrier((*terms, away))
    other = send(away, ZHALF)
    got = [send(term, perm) for term, perm in zip(terms, (PLUS, MINUS, FAR))]
    return own + got[0] + got[1] + got[2] + other


def statistics(grad, weight, row_state, col_state):
    sq = grad * grad + 1e-30
    row_total = sum4(jnp.sum(sq, axis=2), "col", RING4)
    row = DECAY * row_state + (1.0 - DECAY) * row_total / FF
    sums = jnp.concatenate(
        [
            jnp.sum(sq, axis=1),
            jnp.sum(grad * grad / row[:, :, None], axis=1),
            jnp.sum(weight * weight, axis=1),
            jnp.broadcast_to(jnp.sum(row, axis=1)[:, None], (E, COLS)),
        ]
    )
    sums = sum4(sums, "dp", X4)
    sums = sum4(sums, "row", RING4)
    for perm in (CORE, ZHALF):
        sums = sums + send(sums, perm)
    squares, scaled, weights, rows = (sums[E * i : E * i + E] for i in range(4))
    col = DECAY * col_state + (1.0 - DECAY) * squares / D
    row_mean = rows[:, 0] / D
    scalars = jnp.stack([jnp.sum(scaled / col, axis=1), jnp.sum(weights, axis=1)])
    scalars = sum4(scalars, "col", RING4)
    clip = jnp.maximum(1.0, jnp.sqrt(scalars[0] * row_mean / (D * FF)))
    step = 0.3 * jnp.maximum(0.001, jnp.sqrt(scalars[1] / (D * FF)))
    return row, col, row_mean, step / clip


def place_kernel(slabs, where, *refs):
    *arrays, out, held, loaded, stored = refs
    copies = []
    at_row = 0
    for i, (array, start, size) in enumerate(slabs):
        stage = held.at[pl.ds(at_row, size)]
        at_row += size
        target = out.at[pl.ds(pl.multiple_of(where[i], 32), size)]
        copies.append(
            (
                pltpu.make_async_copy(arrays[array].at[pl.ds(start, size)], stage, loaded.at[i]),
                pltpu.make_async_copy(stage, target, stored.at[i]),
            )
        )
    for load, _ in copies:
        load.start()
    for load, store in copies:
        load.wait()
        store.start()
    for _, store in copies:
        store.wait()


def put(out, arrays, slabs, rows):
    any_space = pl.BlockSpec(memory_space=pl.ANY)
    operands = [jnp.stack(rows).astype(jnp.int32)]
    operands += [array.reshape(-1, COLS) for array in arrays]
    aliases = {}
    if out is not None:
        aliases = {len(operands): 0}
        operands.append(out)
    specs = [pl.BlockSpec(memory_space=pltpu.SMEM)] + [any_space] * (len(operands) - 1)
    return pl.pallas_call(
        functools.partial(place_kernel, slabs),
        out_shape=jax.ShapeDtypeStruct((E * 1024, COLS), jnp.float32),
        in_specs=specs,
        out_specs=any_space,
        scratch_shapes=[
            pltpu.VMEM((sum(size for _, _, size in slabs), COLS), jnp.float32),
            pltpu.SemaphoreType.DMA((len(slabs),)),
            pltpu.SemaphoreType.DMA((len(slabs),)),
        ],
        input_output_aliases=aliases,
    )(*operands)


def gather_rows(shard):
    zh, x, c = place()

    def row(dc, expert, dz, dx):
        at_c = (zh + dz) % 2 * 8 + (x + dx) % 4 * 2 + (c + dc) % 2
        return expert * 1024 + ROWS * at_c

    def write(out, pieces):
        arrays, slabs, rows = [], [], []
        for mine, theirs, parts in pieces:
            for dc, array in enumerate((mine, theirs)):
                for i, to in enumerate(parts):
                    slabs.append((len(arrays), i * ROWS, ROWS))
                    rows.append(row(dc, *to))
                arrays.append(array)
        return put(out, arrays, slabs, rows)

    def with_partner(array, parts):
        return array, send(array, CORE), parts

    both = lambda dz, dx: [(e, dz, dx) for e in range(E)]
    other = [send(shard[e], ZHALF) for e in range(E)]
    left, right = send(shard, PLUS), send(shard, MINUS)
    shard_c = send(shard, CORE)

    left, right, other_0, shard_c = lax.optimization_barrier((left, right, other[0], shard_c))
    plus = jnp.concatenate([left[0], other_0])
    minus = jnp.concatenate([right[1], other_0])
    plus, minus = lax.optimization_barrier((plus, minus))
    from_left, from_right, far_0 = send(plus, PLUS), send(minus, MINUS), send(other_0, FAR)

    from_left, from_right, far_0, other_1 = lax.optimization_barrier(
        (from_left, from_right, far_0, other[1])
    )
    left_1, right_1, far_1 = send(other_1, PLUS), send(other_1, MINUS), send(other_1, FAR)
    others = jnp.concatenate([other_0, other_1])
    out = write(
        None,
        [
            (shard, shard_c, both(0, 0)),
            with_partner(left, both(0, 3)),
            with_partner(right, both(0, 1)),
            with_partner(from_left, [(0, 0, 2), (0, 1, 3)]),
            with_partner(from_right, [(1, 0, 2), (0, 1, 1)]),
            with_partner(others, both(1, 0)),
        ],
    )

    out, left_1, right_1, far_1, far_0 = lax.optimization_barrier(
        (out, left_1, right_1, far_1, far_0)
    )
    return write(
        out,
        [
            with_partner(left_1, [(1, 1, 3)]),
            with_partner(right_1, [(1, 1, 1)]),
            with_partner(far_1, [(1, 1, 2)]),
            with_partner(far_0, [(0, 1, 2)]),
        ],
    )


def body(grad_parts, weight, row_state, col_state):
    grad = scatter(grad_parts.reshape(E, 2, 2, 2, 2, ROWS, COLS))
    row, col, row_mean, scale = statistics(grad, weight, row_state, col_state)
    vhat = row[:, :, None] * col[:, None, :] / row_mean[:, None, None]
    new = weight - scale[:, None, None] * (grad / jnp.sqrt(vhat))
    return gather_rows(new).reshape(E, 1024, COLS), row, col


def solution(mesh):
    placed = (
        P("dp", None, "row", "col"),
        P(None, ("row", "dp"), "col"),
        P(None, ("row", "dp")),
        P(None, "col"),
    )
    return jax.shard_map(
        body,
        mesh=mesh,
        in_specs=placed,
        out_specs=(P(None, "row", "col"), P(None, ("row", "dp")), P(None, "col")),
        check_vma=False,
    )
```

```python
import functools

import jax
import jax.numpy as jnp
from jax import lax
from jax.experimental import pallas as pl
from jax.experimental.pallas import tpu as pltpu
from jax.sharding import PartitionSpec as P

D = 4096
FF = 5120
E = 2
ROWS = 64
COLS = 1280
DECAY = 1.0 - 2.0 ** (-0.8)

DP = [(zh, x, c) for zh in range(2) for x in range(4) for c in range(2)]


def at(zh, x, c):
    return (zh % 2) * 8 + (x % 4) * 2 + c % 2


def dp_perm(dz, dx, dc):
    return [(at(zh, x, c), at(zh + dz, x + dx, c + dc)) for zh, x, c in DP]


CORE = dp_perm(0, 0, 1)
PLUS = dp_perm(0, 1, 0)
MINUS = dp_perm(0, -1, 0)
ZHALF = dp_perm(1, 0, 0)
FAR = dp_perm(0, 2, 0)


def send(value, perm):
    return lax.ppermute(value, "dp", perm)


def sum4(value, axis, perms):
    second, third, fourth = (lax.ppermute(value, axis, perm) for perm in perms)
    return (value + third) + (second + fourth)


RING4 = [[(i, (i + k) % 4) for i in range(4)] for k in (1, 2, 3)]
X4 = [dp_perm(0, k, 0) for k in (1, 2, 3)]


def place():
    dp = lax.axis_index("dp")
    return dp // 8, dp // 2 % 4, dp % 2


def after(values, *earlier):
    return lax.optimization_barrier((values, earlier))[0]


def cut(parts, start, size):
    return lax.dynamic_slice(parts, (*start, 0, 0), (*size, ROWS, COLS))


def scatter(parts):
    zh, x, c = place()
    high, low = x // 2, x % 2

    def swap(start, size, *earlier):
        core = after(1 - c, *earlier) if earlier else 1 - c
        return send(cut(parts, (*start, core), (*size, 1)), CORE)

    def block(theirs, expert, half, dx):
        to = (x + dx) % 4
        mine = cut(parts, (expert, half, to // 2, to % 2, c), (1,) * 5)
        return mine.reshape(ROWS, COLS) + theirs.reshape(ROWS, COLS)

    def block_pair(theirs, half, dxs):
        return [block(theirs[e], e, half, dxs[e]) for e in range(E)]

    def sides(swap, half, swapped):
        pick = lambda e, dx: lax.dynamic_index_in_dim(swap[e, 0], (x + dx) % 4 // 2, 0)
        order = (1, 0) if swapped else (0, 1)
        return [block(pick(e, dx), e, half, dx) for e, dx in zip(order, (1, 3))]

    def pair_send(pair):
        return [send(pair[0], PLUS), send(pair[1], MINUS)]

    def finish(far, side_swap, own_swap, half):
        near_rows = sides(side_swap, half, True)
        next_rows = sides(side_swap, half, False)
        rows = after(
            [jnp.concatenate([n, m + f]) for n, m, f in zip(near_rows, next_rows, far)]
        )
        got = pair_send(rows)
        own = block_pair(own_swap, half, (0, 0))
        total = [own[e] + got[1 - e][:ROWS] + got[e][ROWS:] for e in range(E)]
        return rows, after(jnp.stack(total))

    far_a = swap((0, 1 - zh, 1 - high, low), (E, 1, 1, 1))
    far_rows = after(block_pair(far_a, 1 - zh, (2, 2)))
    far = pair_send(far_rows)
    side_a = swap((0, 1 - zh, 0, 1 - low), (E, 1, 2, 1), far_rows)
    own_a = swap((0, 1 - zh, high, low), (E, 1, 1, 1), far_rows)
    rows, away = finish(far, side_a, own_a, 1 - zh)

    def both_experts(dx):
        to = (x + dx) % 4
        start = (0, zh, to // 2, to % 2)
        theirs = swap(start, (E, 1, 1, 1), rows)
        mine = cut(parts, (*start, c), (E, 1, 1, 1, 1))
        return (mine + theirs).reshape(E, ROWS, COLS)

    *terms, own = after([both_experts(dx) for dx in (1, 3, 2, 0)], rows)
    terms[2] = [terms[2][e] for e in range(E)]
    terms, away = lax.optimization_barrier((terms, away))
    other = send(away, ZHALF)
    left, right = send(terms[0], PLUS), send(terms[1], MINUS)
    far = jnp.stack([send(terms[2][e], FAR) for e in range(E)])
    return own + left + right + far + other


def statistics(grad, weight, row_state, col_state):
    sq = grad * grad + 1e-30
    row_total = sum4(jnp.sum(sq, axis=2), "col", RING4)
    row = DECAY * row_state + (1.0 - DECAY) * row_total / FF
    sums = jnp.concatenate(
        [
            jnp.sum(sq, axis=1),
            jnp.sum(grad * grad / row[:, :, None], axis=1),
            jnp.sum(weight * weight, axis=1),
            jnp.broadcast_to(jnp.sum(row, axis=1)[:, None], (E, COLS)),
        ]
    )
    sums = sum4(sums, "dp", X4)
    sums = sum4(sums, "row", RING4)
    for perm in (CORE, ZHALF):
        sums = sums + send(sums, perm)
    squares, scaled, weights, rows = (sums[E * i : E * i + E] for i in range(4))
    col = DECAY * col_state + (1.0 - DECAY) * squares / D
    row_mean = rows[:, 0] / D
    scalars = jnp.stack([jnp.sum(scaled / col, axis=1), jnp.sum(weights, axis=1)])
    scalars = sum4(scalars, "col", RING4)
    clip = jnp.maximum(1.0, jnp.sqrt(scalars[0] * row_mean / (D * FF)))
    step = 0.3 * jnp.maximum(0.001, jnp.sqrt(scalars[1] / (D * FF)))
    return row, col, row_mean, step / clip


def place_kernel(slabs, where, *refs):
    *arrays, out, held, loaded, stored = refs
    copies = []
    at_row = 0
    for i, (array, start, size) in enumerate(slabs):
        stage = held.at[pl.ds(at_row, size)]
        at_row += size
        target = out.at[pl.ds(pl.multiple_of(where[i], 32), size)]
        copies.append(
            (
                pltpu.make_async_copy(arrays[array].at[pl.ds(start, size)], stage, loaded.at[i]),
                pltpu.make_async_copy(stage, target, stored.at[i]),
            )
        )
    for load, _ in copies:
        load.start()
    for load, store in copies:
        load.wait()
        store.start()
    for _, store in copies:
        store.wait()


def put(out, arrays, slabs, rows):
    any_space = pl.BlockSpec(memory_space=pl.ANY)
    operands = [jnp.stack(rows).astype(jnp.int32)]
    operands += [array.reshape(-1, COLS) for array in arrays]
    aliases = {}
    if out is not None:
        aliases = {len(operands): 0}
        operands.append(out)
    specs = [pl.BlockSpec(memory_space=pltpu.SMEM)] + [any_space] * (len(operands) - 1)
    return pl.pallas_call(
        functools.partial(place_kernel, slabs),
        out_shape=jax.ShapeDtypeStruct((E * 1024, COLS), jnp.float32),
        in_specs=specs,
        out_specs=any_space,
        scratch_shapes=[
            pltpu.VMEM((sum(size for _, _, size in slabs), COLS), jnp.float32),
            pltpu.SemaphoreType.DMA((len(slabs),)),
            pltpu.SemaphoreType.DMA((len(slabs),)),
        ],
        input_output_aliases=aliases,
    )(*operands)


def gather_rows(shard):
    zh, x, c = place()

    def row(dc, expert, dz, dx):
        at_c = (zh + dz) % 2 * 8 + (x + dx) % 4 * 2 + (c + dc) % 2
        return expert * 1024 + ROWS * at_c

    def write(out, pieces):
        arrays, slabs, rows = [], [], []
        for mine, theirs, parts in pieces:
            for dc, array in enumerate((mine, theirs)):
                for i, to in enumerate(parts):
                    slabs.append((len(arrays), i * ROWS, ROWS))
                    rows.append(row(dc, *to))
                arrays.append(array)
        return put(out, arrays, slabs, rows)

    def with_partner(array, parts):
        return array, send(array, CORE), parts

    both = lambda dz, dx: [(e, dz, dx) for e in range(E)]
    other = [send(shard[e], ZHALF) for e in range(E)]
    left, right = send(shard, PLUS), send(shard, MINUS)
    shard_c = send(shard, CORE)

    left, right, other_0, shard_c = lax.optimization_barrier((left, right, other[0], shard_c))
    plus = jnp.concatenate([left[0], other_0])
    minus = jnp.concatenate([right[1], other_0])
    plus, minus = lax.optimization_barrier((plus, minus))
    from_left, from_right, far_0 = send(plus, PLUS), send(minus, MINUS), send(other_0, FAR)

    from_left, from_right, far_0, other_1 = lax.optimization_barrier(
        (from_left, from_right, far_0, other[1])
    )
    left_1, right_1, far_1 = send(other_1, PLUS), send(other_1, MINUS), send(other_1, FAR)
    others = jnp.concatenate([other_0, other_1])
    out = write(
        None,
        [
            (shard, shard_c, both(0, 0)),
            with_partner(left, both(0, 3)),
            with_partner(right, both(0, 1)),
            with_partner(from_left, [(0, 0, 2), (0, 1, 3)]),
            with_partner(from_right, [(1, 0, 2), (0, 1, 1)]),
            with_partner(others, both(1, 0)),
        ],
    )

    out, left_1, right_1, far_1, far_0 = lax.optimization_barrier(
        (out, left_1, right_1, far_1, far_0)
    )
    return write(
        out,
        [
            with_partner(left_1, [(1, 1, 3)]),
            with_partner(right_1, [(1, 1, 1)]),
            with_partner(far_1, [(1, 1, 2)]),
            with_partner(far_0, [(0, 1, 2)]),
        ],
    )


def body(grad_parts, weight, row_state, col_state):
    grad = scatter(grad_parts.reshape(E, 2, 2, 2, 2, ROWS, COLS))
    row, col, row_mean, scale = statistics(grad, weight, row_state, col_state)
    vhat = row[:, :, None] * col[:, None, :] / row_mean[:, None, None]
    new = weight - scale[:, None, None] * (grad / jnp.sqrt(vhat))
    return gather_rows(new).reshape(E, 1024, COLS), row, col


def solution(mesh):
    placed = (
        P("dp", None, "row", "col"),
        P(None, ("row", "dp"), "col"),
        P(None, ("row", "dp")),
        P(None, "col"),
    )
    return jax.shard_map(
        body,
        mesh=mesh,
        in_specs=placed,
        out_specs=(P(None, "row", "col"), P(None, ("row", "dp")), P(None, "col")),
        check_vma=False,
    )
```

```python
import functools

import jax
import jax.numpy as jnp
from jax import lax
from jax.experimental import pallas as pl
from jax.experimental.pallas import tpu as pltpu
from jax.sharding import PartitionSpec as P

D = 4096
FF = 5120
E = 2
ROWS = 64
COLS = 1280
DECAY = 1.0 - 2.0 ** (-0.8)

DP = [(zh, x, c) for zh in range(2) for x in range(4) for c in range(2)]


def at(zh, x, c):
    return (zh % 2) * 8 + (x % 4) * 2 + c % 2


def dp_perm(dz, dx, dc):
    return [(at(zh, x, c), at(zh + dz, x + dx, c + dc)) for zh, x, c in DP]


CORE = dp_perm(0, 0, 1)
PLUS = dp_perm(0, 1, 0)
MINUS = dp_perm(0, -1, 0)
ZHALF = dp_perm(1, 0, 0)
FAR = dp_perm(0, 2, 0)


def send(value, perm):
    return lax.ppermute(value, "dp", perm)


def sum4(value, axis, perms):
    second, third, fourth = (lax.ppermute(value, axis, perm) for perm in perms)
    return (value + third) + (second + fourth)


RING4 = [[(i, (i + k) % 4) for i in range(4)] for k in (1, 2, 3)]
X4 = [dp_perm(0, k, 0) for k in (1, 2, 3)]


def place():
    dp = lax.axis_index("dp")
    return dp // 8, dp // 2 % 4, dp % 2


def after(values, *earlier):
    return lax.optimization_barrier((values, earlier))[0]


def cut(parts, start, size):
    return lax.dynamic_slice(parts, (*start, 0, 0), (*size, ROWS, COLS))


def scatter(parts):
    zh, x, c = place()
    high, low = x // 2, x % 2

    def swap(start, size, *earlier):
        core = after(1 - c, *earlier) if earlier else 1 - c
        return send(cut(parts, (*start, core), (*size, 1)), CORE)

    def block(theirs, expert, half, dx):
        to = (x + dx) % 4
        mine = cut(parts, (expert, half, to // 2, to % 2, c), (1,) * 5)
        return mine.reshape(ROWS, COLS) + theirs.reshape(ROWS, COLS)

    def block_pair(theirs, half, dxs):
        return [block(theirs[e], e, half, dxs[e]) for e in range(E)]

    def sides(swap, half, swapped):
        pick = lambda e, dx: lax.dynamic_index_in_dim(swap[e, 0], (x + dx) % 4 // 2, 0)
        order = (1, 0) if swapped else (0, 1)
        return [block(pick(e, dx), e, half, dx) for e, dx in zip(order, (1, 3))]

    def pair_send(pair):
        return [send(pair[0], PLUS), send(pair[1], MINUS)]

    def finish(far, side_swap, own_swap, half):
        near_rows = sides(side_swap, half, True)
        next_rows = sides(side_swap, half, False)
        rows = after(
            [jnp.concatenate([n, m + f]) for n, m, f in zip(near_rows, next_rows, far)]
        )
        got = pair_send(rows)
        own = block_pair(own_swap, half, (0, 0))
        total = [own[e] + got[1 - e][:ROWS] + got[e][ROWS:] for e in range(E)]
        return rows, after(jnp.stack(total))

    far_a = swap((0, 1 - zh, 1 - high, low), (E, 1, 1, 1))
    far_rows = after(block_pair(far_a, 1 - zh, (2, 2)))
    far = pair_send(far_rows)
    side_a = swap((0, 1 - zh, 0, 1 - low), (E, 1, 2, 1), far_rows)
    own_a = swap((0, 1 - zh, high, low), (E, 1, 1, 1), far_rows)
    rows, away = finish(far, side_a, own_a, 1 - zh)

    def both_experts(dx):
        to = (x + dx) % 4
        start = (0, zh, to // 2, to % 2)
        theirs = swap(start, (E, 1, 1, 1), rows)
        mine = cut(parts, (*start, c), (E, 1, 1, 1, 1))
        return (mine + theirs).reshape(E, ROWS, COLS)

    *terms, own = after([both_experts(dx) for dx in (1, 3, 2, 0)], rows)
    terms[2] = [terms[2][e] for e in range(E)]
    terms, away = lax.optimization_barrier((terms, away))
    other = send(away, ZHALF)
    left, right = send(terms[0], PLUS), send(terms[1], MINUS)
    far = jnp.stack([send(terms[2][e], FAR) for e in range(E)])
    return own + left + right + far + other


def statistics(grad, weight, row_state, col_state):
    sq = grad * grad + 1e-30
    row_total = sum4(jnp.sum(sq, axis=2), "col", RING4)
    row = DECAY * row_state + (1.0 - DECAY) * row_total / FF
    sums = jnp.concatenate(
        [
            jnp.sum(sq, axis=1),
            jnp.sum(grad * grad / row[:, :, None], axis=1),
            jnp.sum(weight * weight, axis=1),
            jnp.broadcast_to(jnp.sum(row, axis=1)[:, None], (E, COLS)),
        ]
    )
    sums = sum4(sums, "dp", X4)
    sums = sum4(sums, "row", RING4)
    for perm in (CORE, ZHALF):
        sums = sums + send(sums, perm)
    squares, scaled, weights, rows = (sums[E * i : E * i + E] for i in range(4))
    col = DECAY * col_state + (1.0 - DECAY) * squares / D
    row_mean = rows[:, 0] / D
    scalars = jnp.stack([jnp.sum(scaled / col, axis=1), jnp.sum(weights, axis=1)])
    scalars = sum4(scalars, "col", RING4)
    clip = jnp.maximum(1.0, jnp.sqrt(scalars[0] * row_mean / (D * FF)))
    step = 0.3 * jnp.maximum(0.001, jnp.sqrt(scalars[1] / (D * FF)))
    return row, col, row_mean, step / clip


def place_kernel(slabs, where, *refs):
    *arrays, out, held, loaded, stored = refs
    copies = []
    at_row = 0
    for i, (array, start, size) in enumerate(slabs):
        stage = held.at[pl.ds(at_row, size)]
        at_row += size
        target = out.at[pl.ds(pl.multiple_of(where[i], 32), size)]
        copies.append(
            (
                pltpu.make_async_copy(arrays[array].at[pl.ds(start, size)], stage, loaded.at[i]),
                pltpu.make_async_copy(stage, target, stored.at[i]),
            )
        )
    for load, _ in copies:
        load.start()
    for load, store in copies:
        load.wait()
        store.start()
    for _, store in copies:
        store.wait()


def put(out, arrays, slabs, rows):
    any_space = pl.BlockSpec(memory_space=pl.ANY)
    operands = [jnp.stack(rows).astype(jnp.int32)]
    operands += [array.reshape(-1, COLS) for array in arrays]
    aliases = {}
    if out is not None:
        aliases = {len(operands): 0}
        operands.append(out)
    specs = [pl.BlockSpec(memory_space=pltpu.SMEM)] + [any_space] * (len(operands) - 1)
    return pl.pallas_call(
        functools.partial(place_kernel, slabs),
        out_shape=jax.ShapeDtypeStruct((E * 1024, COLS), jnp.float32),
        in_specs=specs,
        out_specs=any_space,
        scratch_shapes=[
            pltpu.VMEM((sum(size for _, _, size in slabs), COLS), jnp.float32),
            pltpu.SemaphoreType.DMA((len(slabs),)),
            pltpu.SemaphoreType.DMA((len(slabs),)),
        ],
        input_output_aliases=aliases,
    )(*operands)


def gather_rows(shard):
    zh, x, c = place()

    def row(dc, expert, dz, dx):
        at_c = (zh + dz) % 2 * 8 + (x + dx) % 4 * 2 + (c + dc) % 2
        return expert * 1024 + ROWS * at_c

    def write(out, pieces):
        arrays, slabs, rows = [], [], []
        for mine, theirs, parts in pieces:
            for dc, array in enumerate((mine, theirs)):
                for i, to in enumerate(parts):
                    slabs.append((len(arrays), i * ROWS, ROWS))
                    rows.append(row(dc, *to))
                arrays.append(array)
        return put(out, arrays, slabs, rows)

    def with_partner(array, parts):
        return array, send(array, CORE), parts

    both = lambda dz, dx: [(e, dz, dx) for e in range(E)]
    other = [send(shard[e], ZHALF) for e in range(E)]
    left = send(shard, PLUS)
    right = [send(shard[e], MINUS) for e in range(E)]
    shard_c = send(shard, CORE)

    left, right, other_0, shard_c = lax.optimization_barrier((left, right, other[0], shard_c))
    right = jnp.stack(right)
    plus = jnp.concatenate([left[0], other_0])
    minus = jnp.concatenate([right[1], other_0])
    plus, minus = lax.optimization_barrier((plus, minus))
    from_left, from_right, far_0 = send(plus, PLUS), send(minus, MINUS), send(other_0, FAR)

    from_left, from_right, far_0, other_1 = lax.optimization_barrier(
        (from_left, from_right, far_0, other[1])
    )
    left_1, right_1, far_1 = send(other_1, PLUS), send(other_1, MINUS), send(other_1, FAR)
    others = jnp.concatenate([other_0, other_1])
    out = write(
        None,
        [
            (shard, shard_c, both(0, 0)),
            with_partner(left, both(0, 3)),
            with_partner(right, both(0, 1)),
            with_partner(from_left, [(0, 0, 2), (0, 1, 3)]),
            with_partner(from_right, [(1, 0, 2), (0, 1, 1)]),
            with_partner(others, both(1, 0)),
        ],
    )

    out, left_1, right_1, far_1, far_0 = lax.optimization_barrier(
        (out, left_1, right_1, far_1, far_0)
    )
    return write(
        out,
        [
            with_partner(left_1, [(1, 1, 3)]),
            with_partner(right_1, [(1, 1, 1)]),
            with_partner(far_1, [(1, 1, 2)]),
            with_partner(far_0, [(0, 1, 2)]),
        ],
    )


def body(grad_parts, weight, row_state, col_state):
    grad = scatter(grad_parts.reshape(E, 2, 2, 2, 2, ROWS, COLS))
    row, col, row_mean, scale = statistics(grad, weight, row_state, col_state)
    vhat = row[:, :, None] * col[:, None, :] / row_mean[:, None, None]
    new = weight - scale[:, None, None] * (grad / jnp.sqrt(vhat))
    return gather_rows(new).reshape(E, 1024, COLS), row, col


def solution(mesh):
    placed = (
        P("dp", None, "row", "col"),
        P(None, ("row", "dp"), "col"),
        P(None, ("row", "dp")),
        P(None, "col"),
    )
    return jax.shard_map(
        body,
        mesh=mesh,
        in_specs=placed,
        out_specs=(P(None, "row", "col"), P(None, ("row", "dp")), P(None, "col")),
        check_vma=False,
    )
```
